768 devices in a mesh: section: 24 (over z, x_hi), tensor: 32 (over y, x_lo, core).
Axes of the slice: x: 4 (x_hi: 2, x_lo: 2; x = x_hi * 2 + x_lo), y: 8, z: 12, core: 2. Of those that a mesh axis runs over, the one named last changes fastest.
Arguments:
- text: bfloat16 [24, 256, 8192], P('section', 'tensor'), may hold values from -6 to 6
- features: bfloat16 [192, 8192], P(None, 'tensor'), may hold values from -6 to 6
- in_gain: bfloat16 [24, 8192], P('section'), may hold values from 0.5 to 1.5
- w_query: bfloat16 [24, 8192, 4096], P('section', None, 'tensor'), may hold values from -0.0625 to 0.0625
- q_gain: bfloat16 [24, 128], P('section'), may hold values from 0.099609375 to 1.8984375
- w_key_value: bfloat16 [24, 8192, 2048], P('section', 'tensor'), may hold values from -0.0625 to 0.0625
- k_gain: bfloat16 [24, 128], P('section'), may hold values from 0.099609375 to 1.8984375
- tile_count: int32 [2], replicated, may hold values from 1 to 4, as said below
- image_start: int32 [2], replicated, may hold values from 1 to 127
- grad_out: bfloat16 [24, 256, 4096], P('section', None, 'tensor'), may hold values from -6 to 6
Outputs:
- attended: bfloat16 [24, 256, 4096], P('section', None, 'tensor')
- feature_grad: float32 [192, 8192], P('section', 'tensor')
The draws below stay inside these ranges and needn't reach their ends.
Inputs may be any that keep to these rules, and one draw needn't show every extreme that they name: `tile_count`: some sample has 4 tiles.
All inputs are finite; a program needn't handle non-finite values.
Results may differ from the reference program's by a relative error of at most 0.0089.
Values may be sent and summed in bfloat16 or wider, within the bound.
A program may use at most 32 MiB of HBM per device.

```python
import jax
import jax.numpy as jnp
from jax import lax

D = 8192
HEADS = 32
KV_HEADS = 8
HEAD_DIM = 128
TILES = 4
TILE_LEN = 24
TXT_TOK = 128
MB = 2
LAYERS = 24
ROWS = 256
IMG_ALL = 192
N_TENSOR = 32


def draw_tile_count(key, part):
    counts = jax.random.randint(key, (MB,), 1, TILES + 1)
    chosen = jax.random.randint(jax.random.fold_in(key, 7), (), 0, MB)
    return jnp.where(jnp.arange(MB) == chosen, TILES, counts).astype(jnp.int32)


def levels(key, extent, cuts, low, largest):
    level, own = 1.0, jax.random.fold_in(key, 6)
    for axis_at, shards_of in cuts:
        steps = jnp.exp(jax.random.uniform(jax.random.fold_in(own, axis_at), (shards_of,), jnp.float32, low / len(cuts), largest / len(cuts)))
        level = level * jnp.repeat(steps, extent[axis_at] // shards_of).reshape([-1 if axis == axis_at else 1 for axis in range(len(extent))])
    return level


def bell_draw(stream_key, dims, deviation, reach, cuts=(), held_as=jnp.bfloat16):
    entries = jax.random.normal(stream_key, dims, jnp.float32) * deviation
    if len(cuts) > 0:
        entries = levels(stream_key, dims, cuts, -0.22, 0.18) * entries
    return jnp.clip(entries, min=-reach, max=reach).astype(held_as)


def setup_inputs(seed: int = 0) -> dict:
    streams_of = jax.random.split(jax.random.key(seed), 11)
    return {
        "text": bell_draw(streams_of[0], (LAYERS, ROWS, D), 1.0, 6.0, ((0, 24), (1, 32))),
        "features": bell_draw(streams_of[1], (IMG_ALL, D), 1.0, 6.0, ((1, 32),)),
        "in_gain": jnp.clip(1.0 + 0.1 * jax.random.normal(streams_of[2], (LAYERS, D), jnp.float32), 0.5, 1.5).astype(jnp.bfloat16),
        "w_query": bell_draw(streams_of[3], (LAYERS, D, HEADS * HEAD_DIM), D ** -0.5, 0.0625, ((0, 24), (2, 32))),
        "q_gain": jnp.clip(1.0 + 0.18 * jax.random.normal(streams_of[4], (LAYERS, HEAD_DIM), jnp.float32), 0.099609375, 1.8984375).astype(jnp.bfloat16),
        "w_key_value": bell_draw(streams_of[5], (LAYERS, D, 2 * KV_HEADS * HEAD_DIM), D ** -0.5, 0.0625, ((0, 24), (1, 32))),
        "k_gain": jnp.clip(1.0 + 0.18 * jax.random.normal(streams_of[6], (LAYERS, HEAD_DIM), jnp.float32), 0.099609375, 1.8984375).astype(jnp.bfloat16),
        "tile_count": draw_tile_count(jax.random.fold_in(streams_of[10], 71), 0),
        "image_start": jax.random.randint(streams_of[8], (MB,), 1, TXT_TOK).astype(jnp.int32),
        "grad_out": bell_draw(streams_of[9], (LAYERS, ROWS, HEADS * HEAD_DIM), 1.0, 6.0, ((0, 24), (2, 32))),
    }


eps = 1e-05

def rms_scale(values, norm_gain):
    inverse = lax.rsqrt(lax.optimization_barrier(jnp.mean(values * values, axis=-1, keepdims=True)) + eps)
    return values * inverse * norm_gain

def rounded(values):
    return lax.optimization_barrier(values.astype(jnp.bfloat16)).astype(jnp.float32)

def reference(text, features, in_gain, w_query, q_gain, w_key_value, k_gain, tile_count, image_start, grad_out):
    score_scale = HEAD_DIM ** (-0.5)
    group_size = HEADS // KV_HEADS
    block_size = HEADS // N_TENSOR
    per_kv = N_TENSOR // KV_HEADS
    image_slots = TILES * TILE_LEN
    key_live = jnp.arange(image_slots, dtype=jnp.int32)[None, :] < (tile_count * TILE_LEN)[:, None]
    row_live = (jnp.arange(TXT_TOK, dtype=jnp.int32)[None, :] >= image_start[:, None]).astype(jnp.float32)
    row_mask = row_live[:, :, None, None]

    def layer(carry, inputs):
        hidden, layer_gain, weight_q, query_gain, weight_kv, key_gain, upstream_in = inputs
        normed = rms_scale(hidden.astype(jnp.float32), layer_gain.astype(jnp.float32)).astype(jnp.bfloat16)
        raw_q = jnp.dot(normed, weight_q, preferred_element_type=jnp.float32)
        queries = rounded(rms_scale(raw_q.reshape(MB, TXT_TOK, HEADS, HEAD_DIM), query_gain.astype(jnp.float32)))
        kv_full = jnp.dot(features, weight_kv, preferred_element_type=jnp.float32)
        key_raw = kv_full[:, :KV_HEADS * HEAD_DIM].reshape(MB, image_slots, KV_HEADS, HEAD_DIM)
        values = rounded(kv_full[:, KV_HEADS * HEAD_DIM:].reshape(MB, image_slots, KV_HEADS, HEAD_DIM))
        inverse = lax.rsqrt(lax.optimization_barrier(jnp.mean(key_raw * key_raw, axis=-1, keepdims=True)) + eps)
        key_hat = key_raw * inverse
        key_scale = key_gain.astype(jnp.float32)
        normed_keys = rounded(key_hat * key_scale)
        keys_h = jnp.repeat(normed_keys, group_size, axis=2)
        values_h = jnp.repeat(values, group_size, axis=2)
        scores = jnp.einsum('bthd,bjhd->bhtj', queries, keys_h) * score_scale
        exponent = jnp.where(key_live[:, None, None, :], jnp.exp(scores), 0.0)
        probs = exponent / lax.optimization_barrier(jnp.sum(exponent, axis=-1, keepdims=True))
        weights = rounded(probs)
        head_out = jnp.einsum('bhtj,bjhd->bthd', weights, values_h) * row_mask
        attended = head_out.reshape(ROWS, HEADS * HEAD_DIM).astype(jnp.bfloat16)
        upstream = upstream_in.astype(jnp.float32).reshape(MB, TXT_TOK, HEADS, HEAD_DIM) * row_mask
        d_weights = jnp.einsum('bthd,bjhd->bhtj', upstream, values_h)
        d_scores = rounded(probs * (d_weights - lax.optimization_barrier(jnp.sum(probs * d_weights, axis=-1, keepdims=True))) * score_scale)
        d_keys = jnp.einsum('bhtj,bthd->bjhd', d_scores, queries)
        d_values = jnp.einsum('bhtj,bthd->bjhd', weights, upstream)
        d_keys = d_keys.reshape(MB, image_slots, N_TENSOR, block_size, HEAD_DIM).sum(axis=3)
        d_values = d_values.reshape(MB, image_slots, N_TENSOR, block_size, HEAD_DIM).sum(axis=3)
        hat_blocks = jnp.repeat(key_hat, per_kv, axis=2)
        inverse_blocks = jnp.repeat(inverse, per_kv, axis=2)
        scaled = d_keys * key_scale
        d_raw = inverse_blocks * (scaled - hat_blocks * lax.optimization_barrier(jnp.mean(hat_blocks * scaled, axis=-1, keepdims=True)))
        d_raw = rounded(d_raw)
        d_values = rounded(d_values)
        key_sum = d_raw.reshape(MB, image_slots, KV_HEADS, per_kv, HEAD_DIM).sum(axis=3)
        value_sum = d_values.reshape(MB, image_slots, KV_HEADS, per_kv, HEAD_DIM).sum(axis=3)
        d_kv = jnp.concatenate([key_sum.reshape(IMG_ALL, KV_HEADS * HEAD_DIM), value_sum.reshape(IMG_ALL, KV_HEADS * HEAD_DIM)], axis=-1).astype(jnp.bfloat16)
        d_feat = lax.dot_general(d_kv, weight_kv, (((1,), (1,)), ((), ())), preferred_element_type=jnp.float32)
        return (carry + d_feat, attended)
    zeros_start = jnp.zeros((IMG_ALL, D), jnp.float32)
    summed_grad, attended = lax.scan(layer, zeros_start, (text, in_gain, w_query, q_gain, w_key_value, k_gain, grad_out))
    return (attended, summed_grad)
```

```python
import functools

import jax
import jax.numpy as jnp
from jax import lax
from jax.experimental import pallas as pl
from jax.experimental.pallas import tpu as pltpu
from jax.sharding import PartitionSpec as P

KV_HEADS = 8
HEAD_DIM = 128
TILES = 4
TILE_LEN = 24
TXT_TOK = 128
MB = 2
SLOTS = TILES * TILE_LEN
IMG = MB * SLOTS
EPS = 1e-05
Y = 8
LANES = 4
N_TENSOR = Y * LANES
N_SECTION = 24
D = 8192
COLS = 256
QUARTER = IMG // LANES
CHUNK = IMG // N_SECTION
SCALE = HEAD_DIM ** (-0.5)
MESH = pl.DeviceIdType.MESH
F32 = jnp.float32
BF16 = jnp.bfloat16

POSITIONS = [(0, 0), (0, 1)]
for _d in range(1, 5):
    POSITIONS.append((-_d, 0))
    if _d < 4:
        POSITIONS.append((_d, 0))
        POSITIONS.append((-_d, 1))
    POSITIONS.append((_d, 1))
POS = {p: i for i, p in enumerate(POSITIONS)}


def last_of(sign, other):
    return 4 if (sign < 0) == (other == 0) else 3


def dotf(a, b, dims):
    return lax.dot_general(a, b, (dims, ((), ())), preferred_element_type=F32)


def kernel(
    text_ref, feat_ref, ing_ref, wq_hbm, qg_ref, wkv_hbm, kg_ref, tc_ref, is_ref, go_ref,
    att_ref, fg_ref,
    wq, wkv, txt, raw_q, part, p_send, p_recv, csum, up_s, up_r, dn_s, dn_r,
    x_s, x_r, kv, dq_s, dq_r, gath, grad, sec_s, sec_r,
    w_sem, txt_send, txt_recv, gat_send, gat_recv, kv_send, kv_recv, q_send, q_recv, s_send, s_recv,
):
    sec = lax.axis_index("section")
    me = lax.axis_index("tensor")
    y = me // LANES
    lane = me % LANES
    xl = lane // 2
    core = lane % 2

    def tid(y_at, x_at, c_at):
        return y_at * LANES + x_at * 2 + c_at

    sib = tid(y, xl, 1 - core)
    xnb = tid(y, 1 - xl, core)
    diag = tid(y, 1 - xl, 1 - core)
    yup = tid((y + 1) % Y, xl, core)
    ydn = tid((y + Y - 1) % Y, xl, core)

    def dev(t):
        return {"tensor": t, "section": sec}

    started = []

    def send(src, dst, s_sem, r_sem, to):
        copy = pltpu.make_async_remote_copy(
            src_ref=src, dst_ref=dst, send_sem=s_sem, recv_sem=r_sem, device_id=to, device_id_type=MESH
        )
        copy.start()
        started.append(copy)

    def wait_recv(dst, s_sem, r_sem):
        pltpu.make_async_remote_copy(
            src_ref=dst, dst_ref=dst, send_sem=s_sem, recv_sem=r_sem, device_id=dev(sib), device_id_type=MESH
        ).wait_recv()

    barrier = pltpu.get_barrier_semaphore()
    for k in range(1, N_SECTION):
        pl.semaphore_signal(
            barrier, inc=1, device_id={"section": (sec + k) % N_SECTION, "tensor": me}, device_id_type=MESH
        )
    for t in (yup, ydn, xnb, sib, diag):
        pl.semaphore_signal(barrier, inc=1, device_id=dev(t), device_id_type=MESH)

    load_kv = pltpu.make_async_copy(wkv_hbm, wkv, w_sem.at[0])
    load_q = pltpu.make_async_copy(wq_hbm, wq, w_sem.at[1])
    load_kv.start()
    load_q.start()

    own = text_ref[...].astype(F32)
    inv = lax.rsqrt(jnp.mean(own * own, axis=-1, keepdims=True) + EPS)
    txt[me] = (own * inv * ing_ref[...].astype(F32)).astype(BF16)

    load_kv.wait()
    part[...] = jnp.dot(feat_ref[...], wkv[...], preferred_element_type=F32)
    p_send[...] = part[pl.ds(pl.multiple_of((1 - core) * SLOTS, SLOTS), SLOTS), :].astype(BF16)

    pl.semaphore_wait(barrier, N_SECTION - 1 + 5)

    def block(y_at, other, c_at):
        return tid(y_at, xl + other - 2 * xl * other, c_at)

    def at_pos(p, c_at):
        return block((y + p[0] + Y) % Y, p[1], c_at)

    class Gather:
        def __init__(self, buf, s_sem, r_sem):
            self.buf, self.s_sem, self.r_sem = buf, s_sem, r_sem

        def put(self, p, kind, to):
            i = POS[p]
            b = at_pos(p, core)
            slot = {"ring": i, "sib": 16 + i, "x": 32}[kind]
            send(self.buf.at[b], self.buf.at[b], self.s_sem.at[slot], self.r_sem.at[self.target(p, kind)], dev(to))

        def target(self, p, kind):
            if kind == "sib":
                return 16 + POS[p]
            if kind == "x":
                return POS[(0, 1)]
            return None

        def ring(self, p, sign):
            q = (p[0] + sign, p[1])
            b = at_pos(p, core)
            send(
                self.buf.at[b], self.buf.at[b], self.s_sem.at[POS[q]], self.r_sem.at[POS[q]],
                dev(yup if sign < 0 else ydn),
            )

        def begin(self):
            p = (0, 0)
            self.ring(p, -1)
            self.ring(p, 1)
            self.put(p, "x", xnb)
            self.put(p, "sib", sib)

        def arrived(self, p):
            b = at_pos(p, core)
            wait_recv(self.buf.at[b], self.s_sem.at[0], self.r_sem.at[POS[p]])
            if p[0] == 0:
                self.ring(p, -1)
                self.ring(p, 1)
            else:
                sign = -1 if p[0] < 0 else 1
                if abs(p[0]) < last_of(sign, p[1]):
                    self.ring(p, sign)
            self.put(p, "sib", sib)

        def step(self, d):
            for p in POSITIONS:
                if abs(p[0]) == d and p != (0, 0):
                    self.arrived(p)

        def settle(self, d):
            for p in POSITIONS:
                if abs(p[0]) == d:
                    wait_recv(self.buf.at[at_pos(p, 1 - core)], self.s_sem.at[0], self.r_sem.at[16 + POS[p]])

    text_all = Gather(txt, txt_send, txt_recv)
    text_all.begin()
    send(p_send, p_recv, kv_send.at[0], kv_recv.at[0], dev(sib))
    text_all.step(0)

    wait_recv(p_recv, kv_send.at[0], kv_recv.at[0])
    csum[...] = part[pl.ds(pl.multiple_of(core * SLOTS, SLOTS), SLOTS), :] + p_recv[...].astype(F32)

    def head_sum(h):
        at = pl.multiple_of(h * HEAD_DIM, HEAD_DIM)
        return jnp.concatenate(
            [csum[:, pl.ds(at, HEAD_DIM)], csum[:, pl.ds(at + KV_HEADS * HEAD_DIM, HEAD_DIM)]], axis=1
        )

    def kv_up(k):
        val = head_sum((y + 4 - k) % Y)
        if k > 0:
            wait_recv(up_r.at[k - 1], kv_send.at[0], kv_recv.at[k])
            val = val + up_r[k - 1].astype(F32)
        up_s[k] = val.astype(BF16)
        send(up_s.at[k], up_r.at[k], kv_send.at[1 + k], kv_recv.at[1 + k], dev(yup))

    def kv_dn(k):
        val = head_sum((y + Y - 3 + k) % Y)
        if k > 0:
            wait_recv(dn_r.at[k - 1], kv_send.at[0], kv_recv.at[4 + k])
            val = val + dn_r[k - 1].astype(F32)
        dn_s[k] = val.astype(BF16)
        send(dn_s.at[k], dn_r.at[k], kv_send.at[5 + k], kv_recv.at[5 + k], dev(ydn))

    def project(y_list):
        rows = jnp.concatenate(
            [txt[pl.ds(yy * LANES, LANES)].astype(F32).reshape(LANES * 8, D) for yy in y_list], axis=0
        ).astype(BF16)
        res = jnp.dot(rows, wq[...], preferred_element_type=F32)
        for i, yy in enumerate(y_list):
            raw_q[pl.ds(pl.multiple_of(yy * 32, 32), 32), :] = res[i * 32 : i * 32 + 32]

    kv_up(0)
    kv_dn(0)
    text_all.step(1)
    kv_up(1)
    kv_dn(1)
    load_q.wait()
    text_all.settle(0)
    text_all.step(2)
    kv_up(2)
    kv_dn(2)
    text_all.settle(1)
    project([(y + Y - 1) % Y, (y + 1) % Y])
    text_all.step(3)
    kv_up(3)
    text_all.settle(2)
    project([(y + Y - 2) % Y, (y + 2) % Y])
    wait_recv(dn_r.at[2], kv_send.at[0], kv_recv.at[7])
    wait_recv(up_r.at[3], kv_send.at[0], kv_recv.at[4])
    x_s[...] = head_sum(y) + up_r[3].astype(F32) + dn_r[2].astype(F32)
    send(x_s, x_r, kv_send.at[8], kv_recv.at[8], dev(xnb))
    text_all.step(4)
    text_all.settle(3)
    project([(y + Y - 3) % Y, (y + 3) % Y])
    wait_recv(x_r, kv_send.at[0], kv_recv.at[8])
    kv[core] = x_s[...] + x_r[...]
    send(kv.at[core], kv.at[core], kv_send.at[9], kv_recv.at[9], dev(sib))
    text_all.settle(4)
    project([y, (y + 4) % Y])
    wait_recv(kv.at[1 - core], kv_send.at[0], kv_recv.at[9])

    rq = raw_q[...]
    q_all = (rq * lax.rsqrt(jnp.mean(rq * rq, axis=-1, keepdims=True) + EPS) * qg_ref[...].astype(F32)).astype(BF16)
    key_gain = kg_ref[...].astype(F32)
    slot_id = lax.broadcasted_iota(jnp.int32, (SLOTS, TXT_TOK), 0)
    row_id = lax.broadcasted_iota(jnp.int32, (TXT_TOK, HEAD_DIM), 0)
    pieces = []
    for b in range(MB):
        q = q_all[b * TXT_TOK : (b + 1) * TXT_TOK]
        key_raw = kv[b][:, :HEAD_DIM]
        values = kv[b][:, HEAD_DIM:].astype(BF16)
        inverse = lax.rsqrt(jnp.mean(key_raw * key_raw, axis=-1, keepdims=True) + EPS)
        key_hat = key_raw * inverse
        keys = (key_hat * key_gain).astype(BF16)
        row_live = (row_id >= is_ref[b]).astype(F32)
        scores = dotf(keys, q, ((1,), (1,))) * SCALE
        expo = jnp.where(slot_id < tc_ref[b] * TILE_LEN, jnp.exp(scores), 0.0)
        probs = expo / jnp.sum(expo, axis=0, keepdims=True)
        weights = probs.astype(BF16)
        att = dotf(weights, values, ((0,), (0,))) * row_live
        att_ref[pl.ds(b * TXT_TOK, TXT_TOK), :] = att.astype(BF16)
        upstream = (go_ref[pl.ds(b * TXT_TOK, TXT_TOK), :].astype(F32) * row_live).astype(BF16)
        d_weights = dotf(values, upstream, ((1,), (1,)))
        d_scores = (
            probs * (d_weights - jnp.sum(probs * d_weights, axis=0, keepdims=True)) * SCALE
        ).astype(BF16)
        d_keys = jnp.dot(d_scores, q, preferred_element_type=F32)
        d_values = jnp.dot(weights, upstream, preferred_element_type=F32)
        scaled = d_keys * key_gain
        d_raw = inverse * (scaled - key_hat * jnp.mean(key_hat * scaled, axis=-1, keepdims=True))
        pieces.append(jnp.concatenate([d_raw.astype(BF16), d_values.astype(BF16)], axis=1))
    for b in range(MB):
        for half in range(2):
            dq_s[b * 2 + half] = pieces[b][half * QUARTER : (half + 1) * QUARTER]

    for i, (t, k) in enumerate(((xnb, lane + 2 - 4 * xl), (diag, 3 - lane), (sib, lane + 1 - 2 * core))):
        send(dq_s.at[k], dq_r.at[lane], q_send.at[i], q_recv.at[i], dev(t))
    dq_r[lane] = dq_s[lane]
    for i, k in enumerate((lane + 2 - 4 * xl, 3 - lane, lane + 1 - 2 * core)):
        wait_recv(dq_r.at[k], q_send.at[0], q_recv.at[i])
    gath[me] = (
        dq_r[0].astype(F32) + dq_r[1].astype(F32) + dq_r[2].astype(F32) + dq_r[3].astype(F32)
    ).astype(BF16)

    def back(h):
        at = pl.multiple_of(h * HEAD_DIM, HEAD_DIM)
        d_kv = gath[pl.ds(h * LANES, LANES)].reshape(IMG, 2 * HEAD_DIM)
        return dotf(d_kv[:, :HEAD_DIM], wkv[:, pl.ds(at, HEAD_DIM)], ((1,), (1,))) + dotf(
            d_kv[:, HEAD_DIM:], wkv[:, pl.ds(at + KV_HEADS * HEAD_DIM, HEAD_DIM)], ((1,), (1,))
        )

    grad_all = Gather(gath, gat_send, gat_recv)
    grad_all.begin()
    for d in range(0, 5):
        grad_all.step(d)
        if d > 0:
            grad_all.settle(d - 1)
            if d == 1:
                grad[...] = back(y)
            else:
                grad[...] += back((y + Y - (d - 1)) % Y) + back((y + d - 1) % Y)
    grad_all.settle(4)
    total = grad[...] + back((y + 4) % Y)
    grad[...] = total
    sec_s[...] = total.reshape(N_SECTION, CHUNK, COLS).astype(BF16)

    for k in range(1, N_SECTION):
        to = (sec + k) % N_SECTION
        send(
            sec_s.at[to], sec_r.at[sec], s_send.at[k], s_recv.at[k], {"section": to, "tensor": me}
        )
    sec_r[sec] = jnp.zeros((CHUNK, COLS), BF16)
    for k in range(1, N_SECTION):
        wait_recv(sec_r.at[(sec + N_SECTION - k) % N_SECTION], s_send.at[0], s_recv.at[k])
    fg_ref[...] = grad[pl.ds(pl.multiple_of(sec * CHUNK, CHUNK), CHUNK), :] + jnp.sum(
        sec_r[...].astype(F32), axis=0
    )
    for copy in started:
        copy.wait_send()


def shards(
    text, features, in_gain, w_query, q_gain, w_key_value, k_gain, tile_count, image_start, grad_out
):
    vmem = pl.BlockSpec(memory_space=pltpu.VMEM)
    anyw = pl.BlockSpec(memory_space=pl.ANY)
    smem = pl.BlockSpec(memory_space=pltpu.SMEM)
    dma = pltpu.SemaphoreType.DMA
    attended, feature_grad = pl.pallas_call(
        kernel,
        name="cross",
        out_shape=(
            jax.ShapeDtypeStruct((MB * TXT_TOK, HEAD_DIM), BF16),
            jax.ShapeDtypeStruct((CHUNK, COLS), F32),
        ),
        in_specs=[vmem, vmem, vmem, anyw, vmem, anyw, vmem, smem, smem, vmem],
        out_specs=(vmem, vmem),
        scratch_shapes=[
            pltpu.VMEM((D, HEAD_DIM), BF16),
            pltpu.VMEM((COLS, 2 * KV_HEADS * HEAD_DIM), BF16),
            pltpu.VMEM((N_TENSOR, 8, D), BF16),
            pltpu.VMEM((MB * TXT_TOK, HEAD_DIM), F32),
            pltpu.VMEM((IMG, 2 * KV_HEADS * HEAD_DIM), F32),
            pltpu.VMEM((SLOTS, 2 * KV_HEADS * HEAD_DIM), BF16),
            pltpu.VMEM((SLOTS, 2 * KV_HEADS * HEAD_DIM), BF16),
            pltpu.VMEM((SLOTS, 2 * KV_HEADS * HEAD_DIM), F32),
            pltpu.VMEM((4, SLOTS, 2 * HEAD_DIM), BF16),
            pltpu.VMEM((4, SLOTS, 2 * HEAD_DIM), BF16),
            pltpu.VMEM((3, SLOTS, 2 * HEAD_DIM), BF16),
            pltpu.VMEM((3, SLOTS, 2 * HEAD_DIM), BF16),
            pltpu.VMEM((SLOTS, 2 * HEAD_DIM), F32),
            pltpu.VMEM((SLOTS, 2 * HEAD_DIM), F32),
            pltpu.VMEM((MB, SLOTS, 2 * HEAD_DIM), F32),
            pltpu.VMEM((LANES, QUARTER, 2 * HEAD_DIM), BF16),
            pltpu.VMEM((LANES, QUARTER, 2 * HEAD_DIM), BF16),
            pltpu.VMEM((N_TENSOR, QUARTER, 2 * HEAD_DIM), BF16),
            pltpu.VMEM((IMG, COLS), F32),
            pltpu.VMEM((N_SECTION, CHUNK, COLS), BF16),
            pltpu.VMEM((N_SECTION, CHUNK, COLS), BF16),
            dma((2,)),
            dma((33,)),
            dma((32,)),
            dma((33,)),
            dma((32,)),
            dma((10,)),
            dma((10,)),
            dma((3,)),
            dma((3,)),
            dma((N_SECTION,)),
            dma((N_SECTION,)),
        ],
        compiler_params=pltpu.CompilerParams(
            collective_id=0, has_side_effects=True, vmem_limit_bytes=48 * 1024 * 1024
        ),
    )(
        text[0], features, in_gain, w_query[0], q_gain, w_key_value[0], k_gain,
        tile_count, image_start, grad_out[0],
    )
    return (attended[None], feature_grad)


def solution(mesh):
    return jax.shard_map(
        shards,
        mesh=mesh,
        in_specs=(
            P("section", "tensor", None),
            P(None, "tensor"),
            P("section", None),
            P("section", None, "tensor"),
            P("section", None),
            P("section", "tensor", None),
            P("section", None),
            P(),
            P(),
            P("section", None, "tensor"),
        ),
        out_specs=(P("section", None, "tensor"), P("section", "tensor")),
        check_vma=False,
    )
```

```python
import functools

import jax
import jax.numpy as jnp
from jax import lax
from jax.experimental import pallas as pl
from jax.experimental.pallas import tpu as pltpu
from jax.sharding import PartitionSpec as P

KV_HEADS = 8
HEAD_DIM = 128
TILES = 4
TILE_LEN = 24
TXT_TOK = 128
MB = 2
SLOTS = TILES * TILE_LEN
IMG = MB * SLOTS
EPS = 1e-05
Y = 8
LANES = 4
N_TENSOR = Y * LANES
N_SECTION = 24
D = 8192
COLS = 256
QUARTER = IMG // LANES
CHUNK = IMG // N_SECTION
CROSS = 6144
SCALE = HEAD_DIM ** (-0.5)
MESH = pl.DeviceIdType.MESH
F32 = jnp.float32
BF16 = jnp.bfloat16

POSITIONS = [(0, 0), (0, 1)]
for _d in range(1, 5):
    POSITIONS.append((-_d, 0))
    if _d < 4:
        POSITIONS.append((_d, 0))
        POSITIONS.append((-_d, 1))
    POSITIONS.append((_d, 1))
POS = {p: i for i, p in enumerate(POSITIONS)}


def dotf(a, b, dims):
    return lax.dot_general(a, b, (dims, ((), ())), preferred_element_type=F32)


def kernel(
    text_hbm, feat_hbm, ing_hbm, wq_hbm, qg_hbm, wkv_hbm, kg_hbm, tc_hbm, is_hbm, go_hbm,
    att_hbm, fg_hbm,
    text_ref, feat_ref, ing_ref, qg_ref, kg_ref, tc_ref, is_ref, go_ref, att_ref, fg_ref,
    wq, wkv, txt, raw_q, part, p_recv, csum, up_s, up_r, dn_s, dn_r,
    x_s, x_r, kv, dq_s, dq_r, gath, grad, sec_s, sec_r,
    w_sem, txt_send, txt_recv, gat_send, gat_recv, kv_send, kv_recv, q_send, q_recv, s_send, s_recv,
):
    sec = lax.axis_index("section")
    me = lax.axis_index("tensor")
    y = me // LANES
    lane = me % LANES
    xl = lane // 2
    core = lane % 2

    def tid(y_at, x_at, c_at):
        return y_at * LANES + x_at * 2 + c_at

    sib = tid(y, xl, 1 - core)
    xnb = tid(y, 1 - xl, core)
    diag = tid(y, 1 - xl, 1 - core)
    yup = tid((y + 1) % Y, xl, core)
    ydn = tid((y + Y - 1) % Y, xl, core)

    def dev(t):
        return {"tensor": t, "section": sec}

    started = []

    def send(src, dst, s_sem, r_sem, to):
        copy = pltpu.make_async_remote_copy(
            src_ref=src, dst_ref=dst, send_sem=s_sem, recv_sem=r_sem, device_id=to, device_id_type=MESH
        )
        copy.start()
        started.append(copy)

    def wait_recv(dst, s_sem, r_sem):
        pltpu.make_async_remote_copy(
            src_ref=dst, dst_ref=dst, send_sem=s_sem, recv_sem=r_sem, device_id=dev(sib), device_id_type=MESH
        ).wait_recv()

    loads = [
        pltpu.make_async_copy(src, dst, w_sem.at[i])
        for i, (src, dst) in enumerate(
            (
                (text_hbm, text_ref), (ing_hbm, ing_ref), (feat_hbm, feat_ref), (wkv_hbm, wkv), (wq_hbm, wq),
                (go_hbm, go_ref), (qg_hbm, qg_ref), (kg_hbm, kg_ref), (tc_hbm, tc_ref), (is_hbm, is_ref),
            )
        )
    ]
    for load in loads:
        load.start()

    near = [yup, ydn, xnb, sib, diag, tid((y + 4) % Y, 1 - xl, core)]
    near += [tid((y + d) % Y, xl, core) for d in (2, 3, 4, 5, 6)]
    barrier = pltpu.get_barrier_semaphore()
    for k in range(1, N_SECTION):
        pl.semaphore_signal(
            barrier, inc=1, device_id={"section": (sec + k) % N_SECTION, "tensor": me}, device_id_type=MESH
        )
    for t in near:
        pl.semaphore_signal(barrier, inc=1, device_id=dev(t), device_id_type=MESH)

    loads[0].wait()
    loads[1].wait()
    own = text_ref[...].astype(F32)
    inv = lax.rsqrt(jnp.mean(own * own, axis=-1, keepdims=True) + EPS)
    txt[me] = (own * inv * ing_ref[...].astype(F32)).astype(BF16)

    def part_at(c_at):
        return part.at[pl.ds(pl.multiple_of(c_at * SLOTS, SLOTS), SLOTS)]

    pl.semaphore_wait(barrier, N_SECTION - 1 + len(near))

    def block(y_at, other, c_at):
        return tid(y_at, xl + other - 2 * xl * other, c_at)

    def at_pos(p, c_at):
        return block((y + p[0] + Y) % Y, p[1], c_at)

    parts = (pl.ds(0, CROSS), pl.ds(CROSS, D - CROSS))

    def name(d, other):
        return ((-4, 0), (4, 1))[other] if abs(d) == 4 else (d, other)

    def text_ref_at(p, part, c_at):
        return txt.at[at_pos(p, c_at), :, parts[part]]

    def text_send(p, part, slot, r_slot, to):
        ref = text_ref_at(p, part, core)
        send(ref, ref, txt_send.at[slot], txt_recv.at[r_slot], dev(to))

    def text_ring(d, other, part, sign):
        far = d + sign
        if abs(far) > (4 if (sign < 0) == (part == 0) else 3):
            return
        slot = POS[name(far, other)] * 2 + part
        text_send(name(d, other), part, slot, slot, yup if sign < 0 else ydn)

    def text_cross(p, part):
        slot = POS[name(p[0], 1)] * 2 + part
        text_send(p, part, 64 + POS[p] * 2 + part, slot, xnb)

    def text_sib(p, part):
        slot = 32 + POS[p] * 2 + part
        text_send(p, part, slot, slot, sib)

    def text_wait(p, part):
        wait_recv(text_ref_at(p, part, core), txt_send.at[0], txt_recv.at[POS[p] * 2 + part])

    def text_begin():
        text_cross((0, 0), 1)
        for part in range(2):
            text_ring(0, 0, part, -1)
            text_ring(0, 0, part, 1)
        text_cross((0, 0), 0)
        for part in range(2):
            text_sib((0, 0), part)

    def text_crossed(d):
        for p in sorted({name(d, 1), name(-d, 1)}):
            text_wait(p, 0)
            text_sib(p, 0)

    def text_step(d):
        for other, part in ((0, 0), (0, 1), (1, 1)):
            for sign in (-1, 1):
                if d > (4 if (sign < 0) == (part == 0) else 3):
                    continue
                p = name(sign * d, other)
                text_wait(p, part)
                text_ring(sign * d, other, part, sign)
                if part == 0:
                    text_cross(p, 0)
                text_sib(p, part)
        text_crossed(d - 1)

    def text_settle(d):
        for p in POSITIONS:
            if abs(p[0]) == d:
                for part in range(2):
                    wait_recv(
                        text_ref_at(p, part, 1 - core), txt_send.at[0], txt_recv.at[32 + POS[p] * 2 + part]
                    )

    text_begin()

    loads[2].wait()
    loads[3].wait()
    part[...] = jnp.dot(feat_ref[...], wkv[...], preferred_element_type=F32)
    send(part_at(1 - core), p_recv, kv_send.at[0], kv_recv.at[0], dev(sib))
    text_wait((0, 1), 1)
    text_ring(0, 1, 1, -1)
    text_ring(0, 1, 1, 1)
    text_sib((0, 1), 1)

    wait_recv(p_recv, kv_send.at[0], kv_recv.at[0])
    csum[...] = part_at(core)[...] + p_recv[...]

    def head_sum(h):
        at = pl.multiple_of(h * HEAD_DIM, HEAD_DIM)
        return jnp.concatenate(
            [csum[:, pl.ds(at, HEAD_DIM)], csum[:, pl.ds(at + KV_HEADS * HEAD_DIM, HEAD_DIM)]], axis=1
        )

    def kv_up(k):
        val = head_sum((y + 4 - k) % Y)
        if k > 0:
            wait_recv(up_r.at[k - 1], kv_send.at[0], kv_recv.at[k])
            val = val + up_r[k - 1]
        up_s[k] = val
        send(up_s.at[k], up_r.at[k], kv_send.at[1 + k], kv_recv.at[1 + k], dev(yup))

    def kv_dn(k):
        val = head_sum((y + Y - 3 + k) % Y)
        if k > 0:
            wait_recv(dn_r.at[k - 1], kv_send.at[0], kv_recv.at[4 + k])
            val = val + dn_r[k - 1]
        dn_s[k] = val
        send(dn_s.at[k], dn_r.at[k], kv_send.at[5 + k], kv_recv.at[5 + k], dev(ydn))

    def project(y_list):
        rows = jnp.concatenate(
            [txt[pl.ds(yy * LANES, LANES)].astype(F32).reshape(LANES * 8, D) for yy in y_list], axis=0
        ).astype(BF16)
        res = jnp.dot(rows, wq[...], preferred_element_type=F32)
        for i, yy in enumerate(y_list):
            raw_q[pl.ds(pl.multiple_of(yy * 32, 32), 32), :] = res[i * 32 : i * 32 + 32]

    kv_up(0)
    kv_dn(0)
    text_step(1)
    kv_up(1)
    kv_dn(1)
    for load in loads[4:]:
        load.wait()
    text_step(2)
    kv_up(2)
    kv_dn(2)
    text_settle(0)
    text_settle(1)
    project([(y + Y - 1) % Y, (y + 1) % Y])
    text_step(3)
    kv_up(3)
    text_settle(2)
    project([(y + Y - 2) % Y, (y + 2) % Y])
    wait_recv(dn_r.at[2], kv_send.at[0], kv_recv.at[7])
    text_step(4)
    wait_recv(up_r.at[3], kv_send.at[0], kv_recv.at[4])
    x_s[...] = head_sum(y) + up_r[3] + dn_r[2]
    send(x_s, x_r, kv_send.at[8], kv_recv.at[8], dev(xnb))
    text_settle(3)
    project([(y + Y - 3) % Y, (y + 3) % Y])
    text_crossed(4)
    wait_recv(x_r, kv_send.at[0], kv_recv.at[8])
    kv[core] = x_s[...] + x_r[...]
    send(kv.at[core], kv.at[core], kv_send.at[9], kv_recv.at[9], dev(sib))
    text_settle(4)
    project([y, (y + 4) % Y])
    wait_recv(kv.at[1 - core], kv_send.at[0], kv_recv.at[9])

    rq = raw_q[...]
    q_all = (rq * lax.rsqrt(jnp.mean(rq * rq, axis=-1, keepdims=True) + EPS) * qg_ref[...].astype(F32)).astype(BF16)
    key_gain = kg_ref[...].astype(F32)
    slot_id = lax.broadcasted_iota(jnp.int32, (SLOTS, TXT_TOK), 0)
    row_id = lax.broadcasted_iota(jnp.int32, (TXT_TOK, HEAD_DIM), 0)
    pieces = []
    for b in range(MB):
        q = q_all[b * TXT_TOK : (b + 1) * TXT_TOK]
        key_raw = kv[b][:, :HEAD_DIM]
        values = kv[b][:, HEAD_DIM:].astype(BF16)
        inverse = lax.rsqrt(jnp.mean(key_raw * key_raw, axis=-1, keepdims=True) + EPS)
        key_hat = key_raw * inverse
        keys = (key_hat * key_gain).astype(BF16)
        row_live = (row_id >= is_ref[b]).astype(F32)
        scores = dotf(keys, q, ((1,), (1,))) * SCALE
        expo = jnp.where(slot_id < tc_ref[b] * TILE_LEN, jnp.exp(scores), 0.0)
        probs = expo / jnp.sum(expo, axis=0, keepdims=True)
        weights = probs.astype(BF16)
        att = dotf(weights, values, ((0,), (0,))) * row_live
        att_ref[pl.ds(b * TXT_TOK, TXT_TOK), :] = att.astype(BF16)
        upstream = (go_ref[pl.ds(b * TXT_TOK, TXT_TOK), :].astype(F32) * row_live).astype(BF16)
        d_weights = dotf(values, upstream, ((1,), (1,)))
        d_scores = (
            probs * (d_weights - jnp.sum(probs * d_weights, axis=0, keepdims=True)) * SCALE
        ).astype(BF16)
        d_keys = jnp.dot(d_scores, q, preferred_element_type=F32)
        d_values = jnp.dot(weights, upstream, preferred_element_type=F32)
        scaled = d_keys * key_gain
        d_raw = inverse * (scaled - key_hat * jnp.mean(key_hat * scaled, axis=-1, keepdims=True))
        pieces.append(jnp.concatenate([d_raw.astype(BF16), d_values.astype(BF16)], axis=1))
    for b in range(MB):
        for half in range(2):
            dq_s[b * 2 + half] = pieces[b][half * QUARTER : (half + 1) * QUARTER]

    for i, (t, k) in enumerate(((xnb, lane + 2 - 4 * xl), (diag, 3 - lane), (sib, lane + 1 - 2 * core))):
        send(dq_s.at[k], dq_r.at[lane], q_send.at[i], q_recv.at[i], dev(t))
    dq_r[lane] = dq_s[lane]
    for i, k in enumerate((lane + 2 - 4 * xl, 3 - lane, lane + 1 - 2 * core)):
        wait_recv(dq_r.at[k], q_send.at[0], q_recv.at[i])
    gath[me] = (
        dq_r[0].astype(F32) + dq_r[1].astype(F32) + dq_r[2].astype(F32) + dq_r[3].astype(F32)
    ).astype(BF16)

    store_att = pltpu.make_async_copy(att_ref, att_hbm, w_sem.at[10])
    store_att.start()

    def back(h):
        at = pl.multiple_of(h * HEAD_DIM, HEAD_DIM)
        d_kv = gath[pl.ds(h * LANES, LANES)].reshape(IMG, 2 * HEAD_DIM)
        return dotf(d_kv[:, :HEAD_DIM], wkv[:, pl.ds(at, HEAD_DIM)], ((1,), (1,))) + dotf(
            d_kv[:, HEAD_DIM:], wkv[:, pl.ds(at + KV_HEADS * HEAD_DIM, HEAD_DIM)], ((1,), (1,))
        )

    def grad_send(p, slot, r_slot, to):
        ref = gath.at[at_pos(p, core)]
        send(ref, ref, gat_send.at[slot], gat_recv.at[r_slot], dev(to))

    def grad_direct(d, other):
        slot = POS[name(-d, other)]
        grad_send((0, 0), slot, slot, tid((y + d + Y) % Y, xl + other - 2 * xl * other, core))

    def grad_cross(p):
        grad_send(p, 32 + POS[p], POS[name(p[0], 1)], xnb)

    def grad_sib(p):
        grad_send(p, 16 + POS[p], 16 + POS[p], sib)

    def grad_wait(p):
        wait_recv(gath.at[at_pos(p, core)], gat_send.at[0], gat_recv.at[POS[p]])

    def grad_settle(d):
        for p in POSITIONS:
            if abs(p[0]) == d:
                wait_recv(gath.at[at_pos(p, 1 - core)], gat_send.at[0], gat_recv.at[16 + POS[p]])

    for d, other in ((1, 0), (-1, 0), (2, 0), (-2, 0), (3, 0), (-3, 0), (4, 1), (4, 0)):
        grad_direct(d, other)
    grad_cross((0, 0))
    grad_sib((0, 0))
    for d in (1, 2, 3):
        for p in ((-d, 0), (d, 0)):
            grad_wait(p)
            grad_cross(p)
            grad_sib(p)
        for p in sorted({(1 - d, 1), (d - 1, 1)}):
            grad_wait(p)
            grad_sib(p)
    for p in ((-4, 0), (4, 1), (-3, 1), (3, 1)):
        grad_wait(p)
        grad_sib(p)
    grad_settle(0)
    grad[...] = back(y)
    for d in (1, 2):
        grad_settle(d)
        grad[...] += back((y + Y - d) % Y) + back((y + d) % Y)
    grad_settle(4)
    grad[...] += back((y + 4) % Y)
    grad_settle(3)
    total = grad[...] + back((y + Y - 3) % Y) + back((y + 3) % Y)
    grad[...] = total
    sec_s[...] = total.reshape(N_SECTION, CHUNK, COLS).astype(BF16)

    for k in sorted(range(1, N_SECTION), key=lambda k: -min(k, N_SECTION - k)):
        to = (sec + k) % N_SECTION
        send(
            sec_s.at[to], sec_r.at[sec], s_send.at[k], s_recv.at[k], {"section": to, "tensor": me}
        )
    sec_r[sec] = jnp.zeros((CHUNK, COLS), BF16)
    for k in range(1, N_SECTION):
        wait_recv(sec_r.at[(sec + N_SECTION - k) % N_SECTION], s_send.at[0], s_recv.at[k])
    fg_ref[...] = grad[pl.ds(pl.multiple_of(sec * CHUNK, CHUNK), CHUNK), :] + jnp.sum(
        sec_r[...].astype(F32), axis=0
    )
    store_fg = pltpu.make_async_copy(fg_ref, fg_hbm, w_sem.at[11])
    store_fg.start()
    for copy in started:
        copy.wait_send()
    store_att.wait()
    store_fg.wait()


def shards(
    text, features, in_gain, w_query, q_gain, w_key_value, k_gain, tile_count, image_start, grad_out
):
    hbm = pl.BlockSpec(memory_space=pltpu.HBM)
    dma = pltpu.SemaphoreType.DMA
    attended, feature_grad = pl.pallas_call(
        kernel,
        name="cross",
        out_shape=(
            jax.ShapeDtypeStruct((MB * TXT_TOK, HEAD_DIM), BF16),
            jax.ShapeDtypeStruct((CHUNK, COLS), F32),
        ),
        in_specs=[hbm] * 10,
        out_specs=(hbm, hbm),
        scratch_shapes=[
            pltpu.VMEM((8, D), BF16),
            pltpu.VMEM((IMG, COLS), BF16),
            pltpu.VMEM((1, D), BF16),
            pltpu.VMEM((1, HEAD_DIM), BF16),
            pltpu.VMEM((1, HEAD_DIM), BF16),
            pltpu.SMEM((MB,), jnp.int32),
            pltpu.SMEM((MB,), jnp.int32),
            pltpu.VMEM((MB * TXT_TOK, HEAD_DIM), BF16),
            pltpu.VMEM((MB * TXT_TOK, HEAD_DIM), BF16),
            pltpu.VMEM((CHUNK, COLS), F32),
            pltpu.VMEM((D, HEAD_DIM), BF16),
            pltpu.VMEM((COLS, 2 * KV_HEADS * HEAD_DIM), BF16),
            pltpu.VMEM((N_TENSOR, 8, D), BF16),
            pltpu.VMEM((MB * TXT_TOK, HEAD_DIM), F32),
            pltpu.VMEM((IMG, 2 * KV_HEADS * HEAD_DIM), F32),
            pltpu.VMEM((SLOTS, 2 * KV_HEADS * HEAD_DIM), F32),
            pltpu.VMEM((SLOTS, 2 * KV_HEADS * HEAD_DIM), F32),
            pltpu.VMEM((4, SLOTS, 2 * HEAD_DIM), F32),
            pltpu.VMEM((4, SLOTS, 2 * HEAD_DIM), F32),
            pltpu.VMEM((3, SLOTS, 2 * HEAD_DIM), F32),
            pltpu.VMEM((3, SLOTS, 2 * HEAD_DIM), F32),
            pltpu.VMEM((SLOTS, 2 * HEAD_DIM), F32),
            pltpu.VMEM((SLOTS, 2 * HEAD_DIM), F32),
            pltpu.VMEM((MB, SLOTS, 2 * HEAD_DIM), F32),
            pltpu.VMEM((LANES, QUARTER, 2 * HEAD_DIM), BF16),
            pltpu.VMEM((LANES, QUARTER, 2 * HEAD_DIM), BF16),
            pltpu.VMEM((N_TENSOR, QUARTER, 2 * HEAD_DIM), BF16),
            pltpu.VMEM((IMG, COLS), F32),
            pltpu.VMEM((N_SECTION, CHUNK, COLS), BF16),
            pltpu.VMEM((N_SECTION, CHUNK, COLS), BF16),
            dma((12,)),
            dma((96,)),
            dma((64,)),
            dma((48,)),
            dma((32,)),
            dma((10,)),
            dma((10,)),
            dma((3,)),
            dma((3,)),
            dma((N_SECTION,)),
            dma((N_SECTION,)),
        ],
        compiler_params=pltpu.CompilerParams(
            collective_id=0, has_side_effects=True, vmem_limit_bytes=60 * 1024 * 1024
        ),
    )(
        text[0], features, in_gain, w_query[0], q_gain, w_key_value[0], k_gain,
        tile_count, image_start, grad_out[0],
    )
    return (attended[None], feature_grad)


def solution(mesh):
    return jax.shard_map(
        shards,
        mesh=mesh,
        in_specs=(
            P("section", "tensor", None),
            P(None, "tensor"),
            P("section", None),
            P("section", None, "tensor"),
            P("section", None),
            P("section", "tensor", None),
            P("section", None),
            P(),
            P(),
            P("section", None, "tensor"),
        ),
        out_specs=(P("section", None, "tensor"), P("section", "tensor")),
        check_vma=False,
    )
```

```python
import functools

import jax
import jax.numpy as jnp
from jax import lax
from jax.experimental import pallas as pl
from jax.experimental.pallas import tpu as pltpu
from jax.sharding import PartitionSpec as P

KV_HEADS = 8
HEAD_DIM = 128
TILES = 4
TILE_LEN = 24
TXT_TOK = 128
MB = 2
SLOTS = TILES * TILE_LEN
IMG = MB * SLOTS
EPS = 1e-05
Y = 8
LANES = 4
N_TENSOR = Y * LANES
N_SECTION = 24
D = 8192
COLS = 256
QUARTER = IMG // LANES
CHUNK = IMG // N_SECTION
HOPS = 6
CROSS = 6144
SCALE = HEAD_DIM ** (-0.5)
MESH = pl.DeviceIdType.MESH
F32 = jnp.float32
BF16 = jnp.bfloat16

POSITIONS = [(0, 0), (0, 1)]
for _d in range(1, 5):
    POSITIONS.append((-_d, 0))
    if _d < 4:
        POSITIONS.append((_d, 0))
        POSITIONS.append((-_d, 1))
    POSITIONS.append((_d, 1))
POS = {p: i for i, p in enumerate(POSITIONS)}


def dotf(a, b, dims):
    return lax.dot_general(a, b, (dims, ((), ())), preferred_element_type=F32)


def kernel(
    text_hbm, feat_hbm, ing_hbm, wq_hbm, qg_hbm, wkv_hbm, kg_hbm, tc_hbm, is_hbm, go_hbm,
    att_hbm, fg_hbm,
    text_ref, feat_ref, ing_ref, qg_ref, kg_ref, tc_ref, is_ref, go_ref, att_ref, fg_ref,
    wq, wkv, txt, raw_q, part, p_recv, csum, up_s, up_r, dn_s, dn_r,
    x_s, x_r, kv, dq_s, dq_r, gath, grad, sec_s, sec_r,
    w_sem, txt_send, txt_recv, gat_send, gat_recv, kv_send, kv_recv, q_send, q_recv, s_send, s_recv, hop,
):
    sec = lax.axis_index("section")
    me = lax.axis_index("tensor")
    y = me // LANES
    lane = me % LANES
    xl = lane // 2
    core = lane % 2

    def tid(y_at, x_at, c_at):
        return y_at * LANES + x_at * 2 + c_at

    sib = tid(y, xl, 1 - core)
    xnb = tid(y, 1 - xl, core)
    diag = tid(y, 1 - xl, 1 - core)
    yup = tid((y + 1) % Y, xl, core)
    ydn = tid((y + Y - 1) % Y, xl, core)

    def dev(t):
        return {"tensor": t, "section": sec}

    started = []

    def send(src, dst, s_sem, r_sem, to):
        copy = pltpu.make_async_remote_copy(
            src_ref=src, dst_ref=dst, send_sem=s_sem, recv_sem=r_sem, device_id=to, device_id_type=MESH
        )
        copy.start()
        started.append(copy)

    def wait_recv(dst, s_sem, r_sem):
        pltpu.make_async_remote_copy(
            src_ref=dst, dst_ref=dst, send_sem=s_sem, recv_sem=r_sem, device_id=dev(sib), device_id_type=MESH
        ).wait_recv()

    loads = [
        pltpu.make_async_copy(src, dst, w_sem.at[i])
        for i, (src, dst) in enumerate(
            (
                (text_hbm, text_ref), (ing_hbm, ing_ref), (feat_hbm, feat_ref), (wkv_hbm, wkv), (wq_hbm, wq),
                (go_hbm, go_ref), (qg_hbm, qg_ref), (kg_hbm, kg_ref), (tc_hbm, tc_ref), (is_hbm, is_ref),
            )
        )
    ]
    for load in loads:
        load.start()

    near = [yup, ydn, xnb, sib, diag, tid((y + 4) % Y, 1 - xl, core)]
    near += [tid((y + d) % Y, xl, core) for d in (2, 3, 4, 5, 6)]
    barrier = pltpu.get_barrier_semaphore()
    sec_up, sec_dn = (sec + 2) % N_SECTION, (sec + N_SECTION - 2) % N_SECTION
    for to in (sec_up, sec_dn, sec + 1 - 2 * (sec % 2)):
        pl.semaphore_signal(barrier, inc=1, device_id={"section": to, "tensor": me}, device_id_type=MESH)
    for t in near:
        pl.semaphore_signal(barrier, inc=1, device_id=dev(t), device_id_type=MESH)

    loads[0].wait()
    loads[1].wait()
    own = text_ref[...].astype(F32)
    inv = lax.rsqrt(jnp.mean(own * own, axis=-1, keepdims=True) + EPS)
    txt[me] = (own * inv * ing_ref[...].astype(F32)).astype(BF16)

    def part_at(c_at):
        return part.at[pl.ds(pl.multiple_of(c_at * SLOTS, SLOTS), SLOTS)]

    pl.semaphore_wait(barrier, 3 + len(near))

    def section_step(r):
        if r > 0:
            for way in range(2):
                pl.semaphore_wait(hop.at[r - 1, way], 1)
        if r < HOPS:
            for way, to in enumerate((sec_up, sec_dn)):
                pl.semaphore_signal(
                    hop.at[r, way], inc=1, device_id={"section": to, "tensor": me}, device_id_type=MESH
                )


    def block(y_at, other, c_at):
        return tid(y_at, xl + other - 2 * xl * other, c_at)

    def at_pos(p, c_at):
        return block((y + p[0] + Y) % Y, p[1], c_at)

    parts = (pl.ds(0, CROSS), pl.ds(CROSS, D - CROSS))

    def name(d, other):
        return ((-4, 0), (4, 1))[other] if abs(d) == 4 else (d, other)

    def text_ref_at(p, part, c_at):
        return txt.at[at_pos(p, c_at), :, parts[part]]

    def text_send(p, part, slot, r_slot, to):
        ref = text_ref_at(p, part, core)
        send(ref, ref, txt_send.at[slot], txt_recv.at[r_slot], dev(to))

    def text_ring(d, other, part, sign):
        far = d + sign
        if abs(far) > (4 if (sign < 0) == (part == 0) else 3):
            return
        slot = POS[name(far, other)] * 2 + part
        text_send(name(d, other), part, slot, slot, yup if sign < 0 else ydn)

    def text_cross(p, part):
        slot = POS[name(p[0], 1)] * 2 + part
        text_send(p, part, 64 + POS[p] * 2 + part, slot, xnb)

    def text_sib(p, part):
        slot = 32 + POS[p] * 2 + part
        text_send(p, part, slot, slot, sib)

    def text_wait(p, part):
        wait_recv(text_ref_at(p, part, core), txt_send.at[0], txt_recv.at[POS[p] * 2 + part])

    def text_begin():
        text_cross((0, 0), 1)
        for part in range(2):
            text_ring(0, 0, part, -1)
            text_ring(0, 0, part, 1)
        text_cross((0, 0), 0)
        for part in range(2):
            text_sib((0, 0), part)

    def text_crossed(d):
        for p in sorted({name(d, 1), name(-d, 1)}):
            text_wait(p, 0)
            text_sib(p, 0)

    def text_step(d):
        for other, part in ((0, 0), (0, 1), (1, 1)):
            for sign in (-1, 1):
                if d > (4 if (sign < 0) == (part == 0) else 3):
                    continue
                p = name(sign * d, other)
                text_wait(p, part)
                text_ring(sign * d, other, part, sign)
                if part == 0:
                    text_cross(p, 0)
                text_sib(p, part)
        text_crossed(d - 1)

    def text_settle(d):
        for p in POSITIONS:
            if abs(p[0]) == d:
                for part in range(2):
                    wait_recv(
                        text_ref_at(p, part, 1 - core), txt_send.at[0], txt_recv.at[32 + POS[p] * 2 + part]
                    )

    text_begin()

    loads[2].wait()
    loads[3].wait()
    part[...] = jnp.dot(feat_ref[...], wkv[...], preferred_element_type=F32)
    send(part_at(1 - core), p_recv, kv_send.at[0], kv_recv.at[0], dev(sib))
    text_wait((0, 1), 1)
    text_ring(0, 1, 1, -1)
    text_ring(0, 1, 1, 1)
    text_sib((0, 1), 1)

    wait_recv(p_recv, kv_send.at[0], kv_recv.at[0])
    csum[...] = part_at(core)[...] + p_recv[...]

    def head_sum(h):
        at = pl.multiple_of(h * HEAD_DIM, HEAD_DIM)
        return jnp.concatenate(
            [csum[:, pl.ds(at, HEAD_DIM)], csum[:, pl.ds(at + KV_HEADS * HEAD_DIM, HEAD_DIM)]], axis=1
        )

    def kv_up(k):
        val = head_sum((y + 4 - k) % Y)
        if k > 0:
            wait_recv(up_r.at[k - 1], kv_send.at[0], kv_recv.at[k])
            val = val + up_r[k - 1]
        up_s[k] = val
        send(up_s.at[k], up_r.at[k], kv_send.at[1 + k], kv_recv.at[1 + k], dev(yup))

    def kv_dn(k):
        val = head_sum((y + Y - 3 + k) % Y)
        if k > 0:
            wait_recv(dn_r.at[k - 1], kv_send.at[0], kv_recv.at[4 + k])
            val = val + dn_r[k - 1]
        dn_s[k] = val
        send(dn_s.at[k], dn_r.at[k], kv_send.at[5 + k], kv_recv.at[5 + k], dev(ydn))

    def project(y_list):
        rows = jnp.concatenate(
            [txt[pl.ds(yy * LANES, LANES)].astype(F32).reshape(LANES * 8, D) for yy in y_list], axis=0
        ).astype(BF16)
        res = jnp.dot(rows, wq[...], preferred_element_type=F32)
        for i, yy in enumerate(y_list):
            raw_q[pl.ds(pl.multiple_of(yy * 32, 32), 32), :] = res[i * 32 : i * 32 + 32]

    section_step(0)
    kv_up(0)
    kv_dn(0)
    section_step(1)
    text_step(1)
    kv_up(1)
    kv_dn(1)
    for load in loads[4:]:
        load.wait()
    section_step(2)
    text_step(2)
    kv_up(2)
    kv_dn(2)
    text_settle(0)
    text_settle(1)
    project([(y + Y - 1) % Y, (y + 1) % Y])
    section_step(3)
    text_step(3)
    kv_up(3)
    text_settle(2)
    project([(y + Y - 2) % Y, (y + 2) % Y])
    wait_recv(dn_r.at[2], kv_send.at[0], kv_recv.at[7])
    section_step(4)
    text_step(4)
    wait_recv(up_r.at[3], kv_send.at[0], kv_recv.at[4])
    x_s[...] = head_sum(y) + up_r[3] + dn_r[2]
    send(x_s, x_r, kv_send.at[8], kv_recv.at[8], dev(xnb))
    text_settle(3)
    project([(y + Y - 3) % Y, (y + 3) % Y])
    section_step(5)
    text_crossed(4)
    wait_recv(x_r, kv_send.at[0], kv_recv.at[8])
    kv[core] = x_s[...] + x_r[...]
    send(kv.at[core], kv.at[core], kv_send.at[9], kv_recv.at[9], dev(sib))
    text_settle(4)
    project([y, (y + 4) % Y])
    wait_recv(kv.at[1 - core], kv_send.at[0], kv_recv.at[9])

    rq = raw_q[...]
    q_all = (rq * lax.rsqrt(jnp.mean(rq * rq, axis=-1, keepdims=True) + EPS) * qg_ref[...].astype(F32)).astype(BF16)
    key_gain = kg_ref[...].astype(F32)
    slot_id = lax.broadcasted_iota(jnp.int32, (SLOTS, TXT_TOK), 0)
    row_id = lax.broadcasted_iota(jnp.int32, (TXT_TOK, HEAD_DIM), 0)
    pieces = []
    for b in range(MB):
        q = q_all[b * TXT_TOK : (b + 1) * TXT_TOK]
        key_raw = kv[b][:, :HEAD_DIM]
        values = kv[b][:, HEAD_DIM:].astype(BF16)
        inverse = lax.rsqrt(jnp.mean(key_raw * key_raw, axis=-1, keepdims=True) + EPS)
        key_hat = key_raw * inverse
        keys = (key_hat * key_gain).astype(BF16)
        row_live = (row_id >= is_ref[b]).astype(F32)
        scores = dotf(keys, q, ((1,), (1,))) * SCALE
        expo = jnp.where(slot_id < tc_ref[b] * TILE_LEN, jnp.exp(scores), 0.0)
        probs = expo / jnp.sum(expo, axis=0, keepdims=True)
        weights = probs.astype(BF16)
        att = dotf(weights, values, ((0,), (0,))) * row_live
        att_ref[pl.ds(b * TXT_TOK, TXT_TOK), :] = att.astype(BF16)
        upstream = (go_ref[pl.ds(b * TXT_TOK, TXT_TOK), :].astype(F32) * row_live).astype(BF16)
        d_weights = dotf(values, upstream, ((1,), (1,)))
        d_scores = (
            probs * (d_weights - jnp.sum(probs * d_weights, axis=0, keepdims=True)) * SCALE
        ).astype(BF16)
        d_keys = jnp.dot(d_scores, q, preferred_element_type=F32)
        d_values = jnp.dot(weights, upstream, preferred_element_type=F32)
        scaled = d_keys * key_gain
        d_raw = inverse * (scaled - key_hat * jnp.mean(key_hat * scaled, axis=-1, keepdims=True))
        pieces.append(jnp.concatenate([d_raw.astype(BF16), d_values.astype(BF16)], axis=1))
    for b in range(MB):
        for half in range(2):
            dq_s[b * 2 + half] = pieces[b][half * QUARTER : (half + 1) * QUARTER]

    for i, (t, k) in enumerate(((xnb, lane + 2 - 4 * xl), (diag, 3 - lane), (sib, lane + 1 - 2 * core))):
        send(dq_s.at[k], dq_r.at[lane], q_send.at[i], q_recv.at[i], dev(t))
    dq_r[lane] = dq_s[lane]
    for i, k in enumerate((lane + 2 - 4 * xl, 3 - lane, lane + 1 - 2 * core)):
        wait_recv(dq_r.at[k], q_send.at[0], q_recv.at[i])
    gath[me] = (
        dq_r[0].astype(F32) + dq_r[1].astype(F32) + dq_r[2].astype(F32) + dq_r[3].astype(F32)
    ).astype(BF16)

    store_att = pltpu.make_async_copy(att_ref, att_hbm, w_sem.at[10])
    store_att.start()

    def back(h):
        at = pl.multiple_of(h * HEAD_DIM, HEAD_DIM)
        d_kv = gath[pl.ds(h * LANES, LANES)].reshape(IMG, 2 * HEAD_DIM)
        return dotf(d_kv[:, :HEAD_DIM], wkv[:, pl.ds(at, HEAD_DIM)], ((1,), (1,))) + dotf(
            d_kv[:, HEAD_DIM:], wkv[:, pl.ds(at + KV_HEADS * HEAD_DIM, HEAD_DIM)], ((1,), (1,))
        )

    def grad_send(p, slot, r_slot, to):
        ref = gath.at[at_pos(p, core)]
        send(ref, ref, gat_send.at[slot], gat_recv.at[r_slot], dev(to))

    def grad_direct(d, other):
        slot = POS[name(-d, other)]
        grad_send((0, 0), slot, slot, tid((y + d + Y) % Y, xl + other - 2 * xl * other, core))

    def grad_cross(p):
        grad_send(p, 32 + POS[p], POS[name(p[0], 1)], xnb)

    def grad_sib(p):
        grad_send(p, 16 + POS[p], 16 + POS[p], sib)

    def grad_wait(p):
        wait_recv(gath.at[at_pos(p, core)], gat_send.at[0], gat_recv.at[POS[p]])

    def grad_settle(d):
        for p in POSITIONS:
            if abs(p[0]) == d:
                wait_recv(gath.at[at_pos(p, 1 - core)], gat_send.at[0], gat_recv.at[16 + POS[p]])

    for d, other in ((1, 0), (-1, 0), (2, 0), (-2, 0), (3, 0), (-3, 0), (4, 1), (4, 0)):
        grad_direct(d, other)
    grad_cross((0, 0))
    grad_sib((0, 0))
    for d in (1, 2, 3):
        for p in ((-d, 0), (d, 0)):
            grad_wait(p)
            grad_cross(p)
            grad_sib(p)
        for p in sorted({(1 - d, 1), (d - 1, 1)}):
            grad_wait(p)
            grad_sib(p)
    for p in ((-4, 0), (4, 1), (-3, 1), (3, 1)):
        grad_wait(p)
        grad_sib(p)
    grad_settle(0)
    grad[...] = back(y)
    for d in (1, 2):
        grad_settle(d)
        grad[...] += back((y + Y - d) % Y) + back((y + d) % Y)
    grad_settle(4)
    grad[...] += back((y + 4) % Y)
    grad_settle(3)
    total = grad[...] + back((y + Y - 3) % Y) + back((y + 3) % Y)
    grad[...] = total
    sec_s[...] = total.reshape(N_SECTION, CHUNK, COLS).astype(BF16)

    section_step(6)
    for k in sorted(range(1, N_SECTION), key=lambda k: -min(k, N_SECTION - k)):
        to = (sec + k) % N_SECTION
        send(
            sec_s.at[to], sec_r.at[sec], s_send.at[k], s_recv.at[k], {"section": to, "tensor": me}
        )
    sec_r[sec] = jnp.zeros((CHUNK, COLS), BF16)
    for k in range(1, N_SECTION):
        wait_recv(sec_r.at[(sec + N_SECTION - k) % N_SECTION], s_send.at[0], s_recv.at[k])
    fg_ref[...] = grad[pl.ds(pl.multiple_of(sec * CHUNK, CHUNK), CHUNK), :] + jnp.sum(
        sec_r[...].astype(F32), axis=0
    )
    store_fg = pltpu.make_async_copy(fg_ref, fg_hbm, w_sem.at[11])
    store_fg.start()
    for copy in started:
        copy.wait_send()
    store_att.wait()
    store_fg.wait()


def shards(
    text, features, in_gain, w_query, q_gain, w_key_value, k_gain, tile_count, image_start, grad_out
):
    hbm = pl.BlockSpec(memory_space=pltpu.HBM)
    dma = pltpu.SemaphoreType.DMA
    attended, feature_grad = pl.pallas_call(
        kernel,
        name="cross",
        out_shape=(
            jax.ShapeDtypeStruct((MB * TXT_TOK, HEAD_DIM), BF16),
            jax.ShapeDtypeStruct((CHUNK, COLS), F32),
        ),
        in_specs=[hbm] * 10,
        out_specs=(hbm, hbm),
        scratch_shapes=[
            pltpu.VMEM((8, D), BF16),
            pltpu.VMEM((IMG, COLS), BF16),
            pltpu.VMEM((1, D), BF16),
            pltpu.VMEM((1, HEAD_DIM), BF16),
            pltpu.VMEM((1, HEAD_DIM), BF16),
            pltpu.SMEM((MB,), jnp.int32),
            pltpu.SMEM((MB,), jnp.int32),
            pltpu.VMEM((MB * TXT_TOK, HEAD_DIM), BF16),
            pltpu.VMEM((MB * TXT_TOK, HEAD_DIM), BF16),
            pltpu.VMEM((CHUNK, COLS), F32),
            pltpu.VMEM((D, HEAD_DIM), BF16),
            pltpu.VMEM((COLS, 2 * KV_HEADS * HEAD_DIM), BF16),
            pltpu.VMEM((N_TENSOR, 8, D), BF16),
            pltpu.VMEM((MB * TXT_TOK, HEAD_DIM), F32),
            pltpu.VMEM((IMG, 2 * KV_HEADS * HEAD_DIM), F32),
            pltpu.VMEM((SLOTS, 2 * KV_HEADS * HEAD_DIM), F32),
            pltpu.VMEM((SLOTS, 2 * KV_HEADS * HEAD_DIM), F32),
            pltpu.VMEM((4, SLOTS, 2 * HEAD_DIM), F32),
            pltpu.VMEM((4, SLOTS, 2 * HEAD_DIM), F32),
            pltpu.VMEM((3, SLOTS, 2 * HEAD_DIM), F32),
            pltpu.VMEM((3, SLOTS, 2 * HEAD_DIM), F32),
            pltpu.VMEM((SLOTS, 2 * HEAD_DIM), F32),
            pltpu.VMEM((SLOTS, 2 * HEAD_DIM), F32),
            pltpu.VMEM((MB, SLOTS, 2 * HEAD_DIM), F32),
            pltpu.VMEM((LANES, QUARTER, 2 * HEAD_DIM), BF16),
            pltpu.VMEM((LANES, QUARTER, 2 * HEAD_DIM), BF16),
            pltpu.VMEM((N_TENSOR, QUARTER, 2 * HEAD_DIM), BF16),
            pltpu.VMEM((IMG, COLS), F32),
            pltpu.VMEM((N_SECTION, CHUNK, COLS), BF16),
            pltpu.VMEM((N_SECTION, CHUNK, COLS), BF16),
            dma((12,)),
            dma((96,)),
            dma((64,)),
            dma((48,)),
            dma((32,)),
            dma((10,)),
            dma((10,)),
            dma((3,)),
            dma((3,)),
            dma((N_SECTION,)),
            dma((N_SECTION,)),
            pltpu.SemaphoreType.REGULAR((HOPS, 2)),
        ],
        compiler_params=pltpu.CompilerParams(
            collective_id=0, has_side_effects=True, vmem_limit_bytes=60 * 1024 * 1024
        ),
    )(
        text[0], features, in_gain, w_query[0], q_gain, w_key_value[0], k_gain,
        tile_count, image_start, grad_out[0],
    )
    return (attended[None], feature_grad)


def solution(mesh):
    return jax.shard_map(
        shards,
        mesh=mesh,
        in_specs=(
            P("section", "tensor", None),
            P(None, "tensor"),
            P("section", None),
            P("section", None, "tensor"),
            P("section", None),
            P("section", "tensor", None),
            P("section", None),
            P(),
            P(),
            P("section", None, "tensor"),
        ),
        out_specs=(P("section", None, "tensor"), P("section", "tensor")),
        check_vma=False,
    )
```
